512 devices in a mesh: dp: 4 (over x), expert: 128 (over z, y, core).
Axes of the slice: x: 4, y: 4, z: 16, core: 2. Of those that a mesh axis runs over, the one named last changes fastest.
Arguments:
- tokens: bfloat16 [65536, 2048], P(('dp', 'expert')), may hold values from -6 to 6
- hidden_grad: bfloat16 [65536, 1, 768], P(('dp', 'expert')), may hold values from -6 to 6
- gate_prob: float32 [65536, 1], P(('dp', 'expert')), may hold values from 0.2 to 1
- slot_choice: int32 [65536, 1], P(('dp', 'expert')), may hold values from 0 to 127; in each aligned block of 128 rows (0 to 127, 128 to 255, ...) at most 2 rows name the same one
- replica_plan: int32 [128], replicated, may hold values from 0 to 63, as said below
- weights: bfloat16 [64, 2, 2048, 768], P(None, None, ('dp', 'expert')), may hold values from -0.125 to 0.125
Outputs:
- input_grad: bfloat16 [65536, 2048], P(('dp', 'expert'))
- expert_grad: bfloat16 [64, 2, 2048, 768], P(None, None, ('dp', 'expert'))
The draws below stay inside these ranges and needn't reach their ends.
Inputs may be any that keep to these rules, and one draw needn't show every extreme that they name: `slot_choice`: among the tokens of one device no slot is named more than 2 times, and 2 is reached; the picks of one token name different slots. `replica_plan`: every expert is held by at least one slot.
All inputs are finite; a program needn't handle non-finite values.
Results may differ from the reference program's by a relative error of at most 0.007.
Values may be sent and summed in bfloat16 or wider, within the bound.
A program may use at most 64 MiB of HBM per device.

```python
import math
import jax
import jax.numpy as jnp
import numpy as np
from jax import lax

D = 2048
FF = 768
TOK_DEV = 128
PICKS = 1
EXPERTS = 64
SLOTS = 128
TOKENS = 65536
CAP = 2
N_DP = 4
N_EXPERT = 128


def draw_replica_plan(key, part):
    first_key, second_key, third_key = jax.random.split(key, 3)
    hot_count = max(1, EXPERTS // 8)
    favoured = jax.random.permutation(first_key, EXPERTS)[:hot_count]
    extra_slots = favoured[jax.random.randint(second_key, (SLOTS - EXPERTS,), 0, hot_count)]
    layout = jnp.concatenate([jnp.arange(EXPERTS, dtype=jnp.int32), extra_slots.astype(jnp.int32)])
    return jax.random.permutation(third_key, layout).astype(jnp.int32)


def levels(stream_key, shape, shards, low, top_value):
    level = 1.0
    for position, shards_of in shards:
        draws = jax.random.uniform(jax.random.fold_in(jax.random.fold_in(stream_key, 6), position), (shards_of,), jnp.float32, low / len(shards), top_value / len(shards))
        level = level * jnp.repeat(jnp.exp(draws), shape[position] // shards_of).reshape((-1,) + (1,) * (len(shape) - 1 - position))
    return level


def deal_out(rng, own, number, rows, amount, top, reach, skew):
    ranking = jax.random.permutation(rng, amount)
    crowded, usual = load_shares(amount, rows * top, reach, skew, True), load_shares(amount, rows * top, reach, skew, False)
    places = jnp.arange(amount)

    def named(lengths, offset_by):
        used = int((lengths > 0).sum())
        fixed = max(1, used // 4)
        passed = fixed + (places - fixed + offset_by * (used - fixed)) % max(1, amount - fixed)
        return jnp.zeros((amount,), jnp.int32).at[ranking[jnp.where(places < fixed, places, passed)]].set(jnp.asarray(lengths, jnp.int32))

    lengths = jnp.where(number % 4 == 0, named(crowded, number // 4), named(usual, number - number // 4 - 1))
    mixed = jax.random.permutation(jax.random.fold_in(own, 3), amount)
    donor, taker = mixed[0:amount // 2 * 2:2], mixed[1:amount // 2 * 2:2]
    margin = jnp.minimum(lengths[donor] - 1, reach - lengths[taker]) // 2
    margin = jnp.where((donor == ranking[0]) | (taker == ranking[0]) | (lengths[taker] == 0), 0, jnp.maximum(margin, 0))
    passed = jax.random.randint(jax.random.fold_in(own, 4), (amount // 2,), 0, 1 << 20) % (margin + 1)
    lengths = lengths.at[donor].add(-passed).at[taker].add(passed)
    labels = jnp.searchsorted(jnp.cumsum(lengths), jnp.arange(rows * top), side="right").astype(jnp.int32)
    table = labels.reshape(top, rows).T
    table = table[jax.random.permutation(jax.random.fold_in(own, 1), rows)]
    offset_by = jax.random.randint(jax.random.fold_in(own, 2), (rows, 1), 0, top)
    return jnp.take_along_axis(table, (jnp.arange(top)[None, :] + offset_by) % top, axis=1)


def load_shares(count, total, limit, lean, full):
    portions = [(1 << 20) // math.isqrt(grade ** lean) + 1 for grade in range(1, count + 1)]
    largest = limit if full else min(limit, max(-(-total // count), total * portions[0] // sum(portions)))
    least = 1 if total - largest >= count - 1 else 0
    counts, surplus = [largest] + [least] * (count - 1), total - largest - least * (count - 1)
    while surplus > 0:
        free = [i for i in range(1, count) if counts[i] < largest] or [i for i in range(1, count) if counts[i] < limit]
        pool, budget = sum([portions[i] for i in free]), surplus
        for i in free:
            addition = min(limit - counts[i], max(1, budget * portions[i] // pool), surplus)
            counts[i] = counts[i] + addition
            surplus = surplus - addition
    return np.array(counts)


def bell_draw(key, extent, width, limit, shards=(), kind=jnp.bfloat16):
    values = jax.random.normal(key, extent, jnp.float32) * width
    if len(shards) > 0:
        values = levels(key, extent, shards, -0.22, 0.18) * values
    return jnp.clip(values, min=-limit, max=limit).astype(kind)


def setup_inputs(seed: int = 0) -> dict:
    splits = jax.random.split(jax.random.key(seed), 7)
    tokens = bell_draw(splits[0], (TOKENS, D), 1.0, 6.0, ((0, 512),))
    hidden_grad = bell_draw(splits[1], (TOKENS, PICKS, FF), 1.0, 6.0, ((0, 512),))
    gate_prob = jnp.clip(0.2 + 0.8 * jax.random.uniform(splits[2], (TOKENS, PICKS), jnp.float32) ** levels(splits[2], (TOKENS, PICKS), ((0, 512),), -0.2, 0.2), 0.2, 1.0)
    slot_choice_keys = jax.random.split(jax.random.fold_in(splits[3], 1), TOKENS // TOK_DEV)
    slot_choice_turns = jax.random.permutation(jax.random.fold_in(splits[3], 3), TOKENS // TOK_DEV)
    slot_choice = jax.vmap(lambda own, number: deal_out(jax.random.fold_in(splits[3], 2), own, number, TOK_DEV, SLOTS, PICKS, CAP, 2))(slot_choice_keys, slot_choice_turns).reshape((TOKENS, PICKS))
    replica_plan = draw_replica_plan(jax.random.fold_in(splits[6], 71), 0)
    weights = bell_draw(splits[5], (EXPERTS, 2, D, FF), D ** -0.5, 0.125, ((2, 512),))
    return {"tokens": tokens, "hidden_grad": hidden_grad, "gate_prob": gate_prob, "slot_choice": slot_choice, "replica_plan": replica_plan, "weights": weights}


def hidden_terms(inputs, cotangent, weight_pair):
    gate_pre = jnp.dot(inputs, weight_pair[0], preferred_element_type=jnp.float32)
    up_pre = jnp.dot(inputs, weight_pair[1], preferred_element_type=jnp.float32)
    sigma = jax.nn.sigmoid(gate_pre)
    scaled = cotangent.astype(jnp.float32)
    grad_gate = (scaled * up_pre * sigma * (1.0 + gate_pre * (1.0 - sigma))).astype(jnp.bfloat16)
    grad_up = (scaled * gate_pre * sigma).astype(jnp.bfloat16)
    return grad_gate, grad_up


def reference(tokens, hidden_grad, gate_prob, slot_choice, replica_plan, weights):
    row_total = TOKENS * PICKS
    group_rows = TOK_DEV * N_EXPERT * PICKS
    depth_rows = N_EXPERT * CAP
    token_rows = jnp.repeat(tokens, PICKS, axis=0)
    cotangent = (gate_prob[:, :, None] * hidden_grad.astype(jnp.float32)).astype(jnp.bfloat16)
    cotangent = cotangent.reshape(row_total, FF)
    input_pad = jnp.concatenate([token_rows, jnp.zeros((1, D), jnp.bfloat16)], axis=0)
    cotangent_pad = jnp.concatenate([cotangent, jnp.zeros((1, FF), jnp.bfloat16)], axis=0)
    flat_slot = slot_choice.reshape(row_total)
    contract_cols = (((1,), (1,)), ((), ()))
    contract_rows = (((0,), (0,)), ((), ()))

    def visit(running, step_index):
        row_grads, gradients = running
        group_index = step_index // SLOTS
        target = step_index % SLOTS
        lower = (group_index * group_rows).astype(jnp.int32)
        segment = lax.dynamic_slice_in_dim(flat_slot, lower, group_rows)
        found = jnp.nonzero(segment == target, size=depth_rows, fill_value=-1)[0].astype(jnp.int32)
        picked = jnp.where(found < 0, jnp.int32(row_total), found + lower).astype(jnp.int32)
        inputs = input_pad[picked]
        cotangent_rows = cotangent_pad[picked]
        owner = replica_plan[target]
        weight_pair = weights[owner]
        grad_gate, grad_up = hidden_terms(inputs, cotangent_rows, weight_pair)
        term = lax.dot_general(grad_gate, weight_pair[0], contract_cols, preferred_element_type=jnp.float32)
        term = term + lax.dot_general(grad_up, weight_pair[1], contract_cols, preferred_element_type=jnp.float32)
        row_grads = row_grads.at[picked].set(term.astype(jnp.bfloat16))
        products = jnp.stack([
            lax.dot_general(inputs, grad_gate, contract_rows, preferred_element_type=jnp.float32),
            lax.dot_general(inputs, grad_up, contract_rows, preferred_element_type=jnp.float32)])
        rounded_products = lax.optimization_barrier(products.astype(jnp.bfloat16))
        gradients = gradients.at[owner].add(rounded_products.astype(jnp.float32))
        return (row_grads, gradients), None

    start = (jnp.zeros((row_total + 1, D), jnp.bfloat16), jnp.zeros((EXPERTS, 2, D, FF), jnp.float32))
    (row_grads, gradients), unused = lax.scan(visit, start, jnp.arange(N_DP * SLOTS, dtype=jnp.int32))
    input_grad = jnp.sum(row_grads[:row_total].astype(jnp.float32).reshape(TOKENS, PICKS, D), axis=1).astype(jnp.bfloat16)
    expert_grad = (gradients / N_DP).astype(jnp.bfloat16)
    return input_grad, expert_grad
```

```python
import jax
import jax.numpy as jnp
from jax import lax
from jax.sharding import PartitionSpec as P


def per_device(tokens, hidden_grad, gate_prob, slot_choice, replica_plan, weights):
    expert_count = lax.axis_size("expert")
    group_count = lax.axis_size("dp")
    token_count, pick_count = slot_choice.shape
    row_count = token_count * pick_count
    capacity = max(2, 2 * row_count // expert_count)
    depth_rows = expert_count * capacity
    model_width = tokens.shape[1]
    hidden_width = hidden_grad.shape[2]
    expert_total = weights.shape[0]
    shard_rows = weights.shape[2]
    block_rows = shard_rows * expert_count

    chooser = (replica_plan[:, None] == jnp.arange(expert_total, dtype=jnp.int32)[None, :]).astype(
        jnp.bfloat16
    )
    send_weights = jnp.einsum(
        "se,ekdf->skdf", chooser, weights, preferred_element_type=jnp.float32
    ).astype(jnp.bfloat16)
    own_weights = lax.all_to_all(send_weights, "expert", split_axis=0, concat_axis=0, tiled=True)
    own_weights = own_weights.transpose(1, 0, 2, 3).reshape(2, block_rows, hidden_width)
    piece = lax.all_gather(own_weights, "dp", axis=0, tiled=False)

    flat_slot = slot_choice.reshape(row_count)
    slot_member = (flat_slot[:, None] == jnp.arange(expert_count, dtype=jnp.int32)[None, :]).astype(
        jnp.int32
    )
    ranking = jnp.sum((jnp.cumsum(slot_member, axis=0) - 1) * slot_member, axis=1)
    position = flat_slot * capacity + ranking
    scatter_table = (jnp.arange(depth_rows, dtype=jnp.int32)[:, None] == position[None, :]).astype(
        jnp.bfloat16
    )
    token_rows = jnp.repeat(tokens, pick_count, axis=0)
    cotangent = (gate_prob[:, :, None] * hidden_grad.astype(jnp.float32)).astype(jnp.bfloat16)
    cotangent = cotangent.reshape(row_count, hidden_width)
    routed = jnp.concatenate([token_rows, cotangent], axis=1)
    send_rows = jnp.dot(scatter_table, routed, preferred_element_type=jnp.float32).astype(
        jnp.bfloat16
    )
    recv_rows = lax.all_to_all(
        send_rows.reshape(expert_count, capacity, model_width + hidden_width),
        "expert",
        split_axis=0,
        concat_axis=0,
        tiled=True,
    ).reshape(depth_rows, model_width + hidden_width)
    recv_inputs = recv_rows[:, :model_width]
    recv_cotangent = recv_rows[:, model_width:]

    column_blocks = jnp.stack(
        [recv_inputs[:, k * block_rows : (k + 1) * block_rows] for k in range(group_count)]
    )
    all_columns = lax.all_to_all(
        column_blocks, "dp", split_axis=0, concat_axis=0, tiled=True
    ).reshape(group_count * depth_rows, block_rows)

    gate_sum = jnp.zeros((depth_rows, hidden_width), jnp.float32)
    up_sum = jnp.zeros((depth_rows, hidden_width), jnp.float32)
    for k in range(group_count):
        block = recv_inputs[:, k * block_rows : (k + 1) * block_rows]
        gate_sum = gate_sum + jnp.dot(block, piece[k, 0], preferred_element_type=jnp.float32)
        up_sum = up_sum + jnp.dot(block, piece[k, 1], preferred_element_type=jnp.float32)
    sigma = jax.nn.sigmoid(gate_sum)
    scaled = recv_cotangent.astype(jnp.float32)
    grad_gate = (scaled * up_sum * sigma * (1.0 + gate_sum * (1.0 - sigma))).astype(jnp.bfloat16)
    grad_up = (scaled * gate_sum * sigma).astype(jnp.bfloat16)
    grads = jnp.concatenate([grad_gate, grad_up], axis=1)
    all_grads = lax.all_gather(grads, "dp", axis=0, tiled=True)

    contract_cols = (((1,), (1,)), ((), ()))
    row_terms = jnp.concatenate(
        [
            (
                lax.dot_general(
                    grad_gate, piece[k, 0], contract_cols, preferred_element_type=jnp.float32
                )
                + lax.dot_general(
                    grad_up, piece[k, 1], contract_cols, preferred_element_type=jnp.float32
                )
            ).astype(jnp.bfloat16)
            for k in range(group_count)
        ],
        axis=1,
    )
    back_rows = lax.all_to_all(
        row_terms.reshape(expert_count, capacity, model_width),
        "expert",
        split_axis=0,
        concat_axis=0,
        tiled=True,
    ).reshape(depth_rows, model_width)

    summed = lax.dot_general(
        all_columns, all_grads, (((0,), (0,)), ((), ())), preferred_element_type=jnp.float32
    ).astype(jnp.bfloat16)
    pieces = summed.reshape(expert_count, shard_rows, 2, hidden_width).transpose(0, 2, 1, 3)
    gathered = lax.all_to_all(pieces, "expert", split_axis=0, concat_axis=0, tiled=True)
    membership = (
        jnp.arange(expert_total, dtype=jnp.int32)[:, None] == replica_plan[None, :]
    ).astype(jnp.bfloat16)
    expert_grad = jnp.einsum(
        "es,skdf->ekdf", membership, gathered, preferred_element_type=jnp.float32
    )
    expert_grad = (expert_grad / group_count).astype(jnp.bfloat16)

    token_grads = lax.dot_general(
        scatter_table, back_rows, (((0,), (0,)), ((), ())), preferred_element_type=jnp.float32
    )
    input_grad = jnp.sum(token_grads.reshape(token_count, pick_count, model_width), axis=1).astype(
        jnp.bfloat16
    )
    return (input_grad, expert_grad)


def solution(mesh):
    placed = (
        P(("dp", "expert"), None),
        P(("dp", "expert"), None, None),
        P(("dp", "expert"), None),
        P(("dp", "expert"), None),
        P(),
        P(None, None, ("dp", "expert"), None),
    )
    return jax.shard_map(
        per_device,
        mesh=mesh,
        in_specs=placed,
        out_specs=(P(("dp", "expert"), None), P(None, None, ("dp", "expert"), None)),
        check_vma=False,
    )
```

```python
import functools

import jax
import jax.numpy as jnp
from jax import lax
from jax.experimental import pallas as pl
from jax.experimental.pallas import tpu as pltpu
from jax.sharding import PartitionSpec as P


def shift(values, distance):
    size = lax.axis_size("dp")
    return lax.ppermute(values, "dp", [(i, (i + distance) % size) for i in range(size)])


def rotate_columns(values, start_block, block):
    doubled = jnp.concatenate([values, values], axis=1)
    return lax.dynamic_slice_in_dim(doubled, start_block * block, values.shape[1], axis=1)


def one_hot(condition):
    return condition.astype(jnp.bfloat16)


def expert_kernel(count, block, hidden, rows_ref, *refs):
    gate_refs, up_refs = refs[:count], refs[count : 2 * count]
    grads_ref, terms_ref = refs[2 * count :]
    gate_sum, up_sum = 0.0, 0.0
    for i in range(count):
        part = rows_ref[:, i * block : (i + 1) * block]
        gate_sum = gate_sum + jnp.dot(part, gate_refs[i][...], preferred_element_type=jnp.float32)
        up_sum = up_sum + jnp.dot(part, up_refs[i][...], preferred_element_type=jnp.float32)
    sigma = 1.0 / (1.0 + jnp.exp(-gate_sum))
    scaled = rows_ref[:, count * block :].astype(jnp.float32)
    grad_gate = (scaled * up_sum * sigma * (1.0 + gate_sum * (1.0 - sigma))).astype(jnp.bfloat16)
    grad_up = (scaled * gate_sum * sigma).astype(jnp.bfloat16)
    grads_ref[:, :hidden] = grad_gate
    grads_ref[:, hidden:] = grad_up
    contract_cols = (((1,), (1,)), ((), ()))
    for i in range(count):
        terms_ref[:, i * block : (i + 1) * block] = (
            lax.dot_general(
                grad_gate, gate_refs[i][...], contract_cols, preferred_element_type=jnp.float32
            )
            + lax.dot_general(
                grad_up, up_refs[i][...], contract_cols, preferred_element_type=jnp.float32
            )
        ).astype(jnp.bfloat16)


def expert_rows(rows, gate_blocks, up_blocks):
    count = len(gate_blocks)
    block, hidden = gate_blocks[0].shape
    depth = rows.shape[0]
    in_vmem = pl.BlockSpec(memory_space=pltpu.VMEM)
    return pl.pallas_call(
        functools.partial(expert_kernel, count, block, hidden),
        out_shape=(
            jax.ShapeDtypeStruct((depth, 2 * hidden), jnp.bfloat16),
            jax.ShapeDtypeStruct((depth, count * block), jnp.bfloat16),
        ),
        in_specs=[in_vmem] * (1 + 2 * count),
        out_specs=(in_vmem, in_vmem),
        compiler_params=pltpu.CompilerParams(vmem_limit_bytes=32 << 20),
        cost_estimate=pl.CostEstimate(
            flops=8 * depth * hidden * count * block,
            bytes_accessed=4 * hidden * count * block + 4 * depth * (count * block + hidden),
            transcendentals=depth * hidden,
        ),
    )(rows, *gate_blocks, *up_blocks)


def per_device(tokens, hidden_grad, gate_prob, slot_choice, replica_plan, weights):
    expert_count = lax.axis_size("expert")
    group_count = lax.axis_size("dp")
    me = lax.axis_index("dp")
    token_count, pick_count = slot_choice.shape
    row_count = token_count * pick_count
    capacity = max(2, 2 * row_count // expert_count)
    depth_rows = expert_count * capacity
    model_width = tokens.shape[1]
    hidden_width = hidden_grad.shape[2]
    expert_total = weights.shape[0]
    shard_rows = weights.shape[2]
    block_rows = shard_rows * expert_count
    routed_width = model_width + hidden_width

    slots = jnp.arange(expert_count, dtype=jnp.int32)
    chooser = one_hot(replica_plan[:, None] == jnp.arange(expert_total, dtype=jnp.int32)[None, :])
    send_weights = jnp.einsum(
        "se,ekdf->skdf", chooser, weights, preferred_element_type=jnp.float32
    ).astype(jnp.bfloat16)
    own = lax.all_to_all(send_weights, "expert", split_axis=0, concat_axis=0, tiled=True)
    own_gate = own[:, 0].reshape(block_rows, hidden_width)
    own_up = own[:, 1].reshape(block_rows, hidden_width)
    left_gate = shift(own_gate, 1)
    right_up = shift(own_up, -1)
    left_up = shift(own_up, 1)
    right_gate = shift(own_gate, -1)
    far_gate = shift(left_gate, 1)
    far_up = shift(right_up, -1)
    gate_blocks = [own_gate, right_gate, far_gate, left_gate]
    up_blocks = [own_up, right_up, far_up, left_up]

    flat_slot = slot_choice.reshape(row_count)
    slot_member = (flat_slot[:, None] == slots[None, :]).astype(jnp.int32)
    ranking = jnp.sum((jnp.cumsum(slot_member, axis=0) - 1) * slot_member, axis=1)
    position = flat_slot * capacity + ranking
    scatter_table = one_hot(jnp.arange(depth_rows, dtype=jnp.int32)[:, None] == position[None, :])
    token_rows = jnp.repeat(rotate_columns(tokens, me, block_rows), pick_count, axis=0)
    cotangent = (gate_prob[:, :, None] * hidden_grad.astype(jnp.float32)).astype(jnp.bfloat16)
    cotangent = cotangent.reshape(row_count, hidden_width)
    routed = jnp.concatenate([token_rows, cotangent], axis=1)
    send_rows = jnp.dot(scatter_table, routed, preferred_element_type=jnp.float32).astype(
        jnp.bfloat16
    )
    send_rows, _ = lax.optimization_barrier(
        (send_rows.reshape(expert_count, capacity, routed_width), own)
    )
    rows = lax.all_to_all(
        send_rows, "expert", split_axis=0, concat_axis=0, tiled=True
    ).reshape(depth_rows, routed_width)

    grads, row_terms = expert_rows(rows, gate_blocks, up_blocks)
    back_rows = lax.all_to_all(
        row_terms.reshape(expert_count, capacity, model_width),
        "expert",
        split_axis=0,
        concat_axis=0,
        tiled=True,
    ).reshape(depth_rows, model_width)

    blocks = [rows[:, i * block_rows : (i + 1) * block_rows] for i in range(group_count)]
    columns = [blocks[0], shift(blocks[3], -1), shift(blocks[2], 2), shift(blocks[1], 1)]
    grads_left = shift(grads, 1)
    grads_right = shift(grads, -1)
    middle = depth_rows // 2
    grads_far = [shift(grads_left[:middle], 1), shift(grads_right[middle:], -1)]
    all_columns = jnp.concatenate(columns, axis=0)
    all_grads = jnp.concatenate([grads, grads_right, *grads_far, grads_left], axis=0)
    contract_rows = (((0,), (0,)), ((), ()))
    summed = lax.dot_general(
        all_columns, all_grads, contract_rows, preferred_element_type=jnp.float32
    ).astype(jnp.bfloat16)
    pieces = summed.reshape(expert_count, shard_rows, 2, hidden_width).transpose(0, 2, 1, 3)
    gathered = lax.all_to_all(pieces, "expert", split_axis=0, concat_axis=0, tiled=True)
    membership = one_hot(
        jnp.arange(expert_total, dtype=jnp.int32)[:, None] == replica_plan[None, :]
    )
    expert_grad = jnp.einsum(
        "es,skdf->ekdf", membership, gathered, preferred_element_type=jnp.float32
    )
    expert_grad = (expert_grad / group_count).astype(jnp.bfloat16)

    token_grads = lax.dot_general(
        scatter_table, back_rows, contract_rows, preferred_element_type=jnp.float32
    )
    input_grad = jnp.sum(token_grads.reshape(token_count, pick_count, model_width), axis=1).astype(
        jnp.bfloat16
    )
    input_grad = rotate_columns(input_grad, (group_count - me) % group_count, block_rows)
    return (input_grad, expert_grad)


def solution(mesh):
    placed = (
        P(("dp", "expert"), None),
        P(("dp", "expert"), None, None),
        P(("dp", "expert"), None),
        P(("dp", "expert"), None),
        P(),
        P(None, None, ("dp", "expert"), None),
    )
    return jax.shard_map(
        per_device,
        mesh=mesh,
        in_specs=placed,
        out_specs=(P(("dp", "expert"), None), P(None, None, ("dp", "expert"), None)),
        check_vma=False,
    )
```

```python
import functools

import jax
import jax.numpy as jnp
from jax import lax
from jax.experimental import pallas as pl
from jax.experimental.pallas import tpu as pltpu
from jax.sharding import PartitionSpec as P


def shift(values, distance):
    size = lax.axis_size("dp")
    return lax.ppermute(values, "dp", [(i, (i + distance) % size) for i in range(size)])


def rotate_columns(values, start_block, block):
    doubled = jnp.concatenate([values, values], axis=1)
    return lax.dynamic_slice_in_dim(doubled, start_block * block, values.shape[1], axis=1)


def one_hot(condition):
    return condition.astype(jnp.bfloat16)


def expert_kernel(count, block, hidden, rows_ref, *refs):
    gate_refs, up_refs = refs[:count], refs[count : 2 * count]
    grads_ref, terms_ref = refs[2 * count :]
    gate_sum, up_sum = 0.0, 0.0
    for i in range(count):
        part = rows_ref[:, i * block : (i + 1) * block]
        gate_sum = gate_sum + jnp.dot(part, gate_refs[i][...], preferred_element_type=jnp.float32)
        up_sum = up_sum + jnp.dot(part, up_refs[i][...], preferred_element_type=jnp.float32)
    sigma = 1.0 / (1.0 + jnp.exp(-gate_sum))
    scaled = rows_ref[:, count * block :].astype(jnp.float32)
    grad_gate = (scaled * up_sum * sigma * (1.0 + gate_sum * (1.0 - sigma))).astype(jnp.bfloat16)
    grad_up = (scaled * gate_sum * sigma).astype(jnp.bfloat16)
    grads_ref[:, :hidden] = grad_gate
    grads_ref[:, hidden:] = grad_up
    contract_cols = (((1,), (1,)), ((), ()))
    for i in range(count):
        terms_ref[:, i * block : (i + 1) * block] = (
            lax.dot_general(
                grad_gate, gate_refs[i][...], contract_cols, preferred_element_type=jnp.float32
            )
            + lax.dot_general(
                grad_up, up_refs[i][...], contract_cols, preferred_element_type=jnp.float32
            )
        ).astype(jnp.bfloat16)


def expert_rows(rows, gate_blocks, up_blocks):
    count = len(gate_blocks)
    block, hidden = gate_blocks[0].shape
    depth = rows.shape[0]
    in_vmem = pl.BlockSpec(memory_space=pltpu.VMEM)
    return pl.pallas_call(
        functools.partial(expert_kernel, count, block, hidden),
        out_shape=(
            jax.ShapeDtypeStruct((depth, 2 * hidden), jnp.bfloat16),
            jax.ShapeDtypeStruct((depth, count * block), jnp.bfloat16),
        ),
        in_specs=[in_vmem] * (1 + 2 * count),
        out_specs=(in_vmem, in_vmem),
        compiler_params=pltpu.CompilerParams(vmem_limit_bytes=32 << 20),
        cost_estimate=pl.CostEstimate(
            flops=8 * depth * hidden * count * block,
            bytes_accessed=4 * hidden * count * block + 4 * depth * (count * block + hidden),
            transcendentals=depth * hidden,
        ),
    )(rows, *gate_blocks, *up_blocks)


PLANE = 8


def exchange_kernel(
    total, send_ref, recv_ref, relay_ref, self_sem, send_sem, recv_sem, out_sem, in_sem, pass_sem
):
    me = lax.axis_index("expert")
    planes, half = total // PLANE, PLANE // 2
    plane, seat = me // PLANE, me % PLANE

    def device(step, place):
        return ((plane + step + planes) % planes) * PLANE + place

    def send(target):
        pltpu.make_async_remote_copy(
            src_ref=send_ref.at[target],
            dst_ref=recv_ref.at[me],
            send_sem=send_sem,
            recv_sem=recv_sem,
            device_id={"expert": target},
            device_id_type=pl.DeviceIdType.MESH,
        ).start()

    barrier = pltpu.get_barrier_semaphore()

    def greet(step, carry):
        pl.semaphore_signal(
            barrier,
            inc=1,
            device_id={"expert": (me + step) % total},
            device_id_type=pl.DeviceIdType.MESH,
        )
        return carry

    lax.fori_loop(1, total, greet, 0)
    pl.semaphore_wait(barrier, total - 1)

    relay = pltpu.make_async_remote_copy(
        src_ref=send_ref.at[pl.ds(device(planes // 2, half), half)],
        dst_ref=relay_ref,
        send_sem=out_sem,
        recv_sem=in_sem,
        device_id={"expert": device(-(planes // 4), seat)},
        device_id_type=pl.DeviceIdType.MESH,
    )
    relay.start()
    for place in range(half):
        send(device(planes // 2, place))
    own = pltpu.make_async_copy(send_ref.at[me], recv_ref.at[me], self_sem)
    own.start()

    def both_ways(item, carry):
        step = planes // 2 - 1 - item // PLANE
        place = (seat + item) % PLANE
        send(device(step, place))
        send(device(-step, place))
        return carry

    def same_plane(step, carry):
        send(device(0, (seat + step) % PLANE))
        return carry

    pairs = (planes // 2 - 1) * PLANE
    lax.fori_loop(0, pairs // 2, both_ways, 0)
    relay.wait_recv()
    source = device(planes // 4, seat)
    for place in range(half):
        pltpu.make_async_remote_copy(
            src_ref=relay_ref.at[place],
            dst_ref=recv_ref.at[source],
            send_sem=pass_sem,
            recv_sem=recv_sem,
            device_id={"expert": device(-(planes // 4), half + place)},
            device_id_type=pl.DeviceIdType.MESH,
        ).start()
    lax.fori_loop(pairs // 2, pairs, both_ways, 0)
    lax.fori_loop(1, PLANE, same_plane, 0)

    own.wait()
    relay.wait_send()
    pltpu.make_async_copy(relay_ref, relay_ref, pass_sem).wait()
    sent = send_ref.at[pl.ds(0, total - 1 - half)]
    pltpu.make_async_copy(sent, sent, send_sem).wait()
    landed = recv_ref.at[pl.ds(0, total - 1)]
    pltpu.make_async_copy(landed, landed, recv_sem).wait()


def exchange(pieces):
    total = pieces.shape[0]
    in_place = pl.BlockSpec(memory_space=pl.ANY)
    return pl.pallas_call(
        functools.partial(exchange_kernel, total),
        out_shape=jax.ShapeDtypeStruct(pieces.shape, pieces.dtype),
        in_specs=[in_place],
        out_specs=in_place,
        scratch_shapes=[pltpu.VMEM((PLANE // 2, *pieces.shape[1:]), pieces.dtype)]
        + [pltpu.SemaphoreType.DMA] * 6,
        compiler_params=pltpu.CompilerParams(
            collective_id=0, has_side_effects=True, vmem_limit_bytes=4 << 20
        ),
    )(pieces)


def per_device(tokens, hidden_grad, gate_prob, slot_choice, replica_plan, weights):
    expert_count = lax.axis_size("expert")
    group_count = lax.axis_size("dp")
    me = lax.axis_index("dp")
    token_count, pick_count = slot_choice.shape
    row_count = token_count * pick_count
    capacity = max(2, 2 * row_count // expert_count)
    depth_rows = expert_count * capacity
    model_width = tokens.shape[1]
    hidden_width = hidden_grad.shape[2]
    expert_total = weights.shape[0]
    shard_rows = weights.shape[2]
    block_rows = shard_rows * expert_count
    routed_width = model_width + hidden_width

    slots = jnp.arange(expert_count, dtype=jnp.int32)
    chooser = one_hot(replica_plan[:, None] == jnp.arange(expert_total, dtype=jnp.int32)[None, :])
    send_weights = jnp.einsum(
        "se,ekdf->skdf", chooser, weights, preferred_element_type=jnp.float32
    ).astype(jnp.bfloat16)
    own = lax.all_to_all(send_weights, "expert", split_axis=0, concat_axis=0, tiled=True)
    own_gate = own[:, 0].reshape(block_rows, hidden_width)
    own_up = own[:, 1].reshape(block_rows, hidden_width)
    left_gate = shift(own_gate, 1)
    right_up = shift(own_up, -1)
    left_up = shift(own_up, 1)
    right_gate = shift(own_gate, -1)
    far_gate = shift(left_gate, 1)
    far_up = shift(right_up, -1)
    gate_blocks = [own_gate, right_gate, far_gate, left_gate]
    up_blocks = [own_up, right_up, far_up, left_up]

    flat_slot = slot_choice.reshape(row_count)
    slot_member = (flat_slot[:, None] == slots[None, :]).astype(jnp.int32)
    ranking = jnp.sum((jnp.cumsum(slot_member, axis=0) - 1) * slot_member, axis=1)
    position = flat_slot * capacity + ranking
    scatter_table = one_hot(jnp.arange(depth_rows, dtype=jnp.int32)[:, None] == position[None, :])
    token_rows = jnp.repeat(rotate_columns(tokens, me, block_rows), pick_count, axis=0)
    cotangent = (gate_prob[:, :, None] * hidden_grad.astype(jnp.float32)).astype(jnp.bfloat16)
    cotangent = cotangent.reshape(row_count, hidden_width)
    routed = jnp.concatenate([token_rows, cotangent], axis=1)
    send_rows = jnp.dot(scatter_table, routed, preferred_element_type=jnp.float32).astype(
        jnp.bfloat16
    )
    send_rows, _ = lax.optimization_barrier(
        (send_rows.reshape(expert_count, capacity, routed_width), own)
    )
    rows = lax.all_to_all(
        send_rows, "expert", split_axis=0, concat_axis=0, tiled=True
    ).reshape(depth_rows, routed_width)

    grads, row_terms = expert_rows(rows, gate_blocks, up_blocks)
    back_rows = lax.all_to_all(
        row_terms.reshape(expert_count, capacity, model_width),
        "expert",
        split_axis=0,
        concat_axis=0,
        tiled=True,
    ).reshape(depth_rows, model_width)

    blocks = [rows[:, i * block_rows : (i + 1) * block_rows] for i in range(group_count)]
    columns = [blocks[0], shift(blocks[3], -1), shift(blocks[2], 2), shift(blocks[1], 1)]
    grads_left = shift(grads, 1)
    grads_right = shift(grads, -1)
    middle = depth_rows // 2
    grads_far = [shift(grads_left[:middle], 1), shift(grads_right[middle:], -1)]
    all_columns = jnp.concatenate(columns, axis=0)
    all_grads = jnp.concatenate([grads, grads_right, *grads_far, grads_left], axis=0)
    contract_rows = (((0,), (0,)), ((), ()))
    summed = lax.dot_general(
        all_columns, all_grads, contract_rows, preferred_element_type=jnp.float32
    ).astype(jnp.bfloat16)
    pieces = summed.reshape(expert_count, shard_rows, 2, hidden_width).transpose(0, 2, 1, 3)
    gathered = exchange(pieces)
    membership = one_hot(
        jnp.arange(expert_total, dtype=jnp.int32)[:, None] == replica_plan[None, :]
    )
    expert_grad = jnp.einsum(
        "es,skdf->ekdf", membership, gathered, preferred_element_type=jnp.float32
    )
    expert_grad = (expert_grad / group_count).astype(jnp.bfloat16)

    token_grads = lax.dot_general(
        scatter_table, back_rows, contract_rows, preferred_element_type=jnp.float32
    )
    input_grad = jnp.sum(token_grads.reshape(token_count, pick_count, model_width), axis=1).astype(
        jnp.bfloat16
    )
    input_grad = rotate_columns(input_grad, (group_count - me) % group_count, block_rows)
    return (input_grad, expert_grad)


def solution(mesh):
    placed = (
        P(("dp", "expert"), None),
        P(("dp", "expert"), None, None),
        P(("dp", "expert"), None),
        P(("dp", "expert"), None),
        P(),
        P(None, None, ("dp", "expert"), None),
    )
    return jax.shard_map(
        per_device,
        mesh=mesh,
        in_specs=placed,
        out_specs=(P(("dp", "expert"), None), P(None, None, ("dp", "expert"), None)),
        check_vma=False,
    )
```

```python
import functools

import jax
import jax.numpy as jnp
from jax import lax
from jax.experimental import pallas as pl
from jax.experimental.pallas import tpu as pltpu
from jax.sharding import PartitionSpec as P


def shift(values, distance):
    size = lax.axis_size("dp")
    return lax.ppermute(values, "dp", [(i, (i + distance) % size) for i in range(size)])


def rotate_columns(values, start_block, block):
    doubled = jnp.concatenate([values, values], axis=1)
    return lax.dynamic_slice_in_dim(doubled, start_block * block, values.shape[1], axis=1)


def one_hot(condition):
    return condition.astype(jnp.bfloat16)


def expert_kernel(count, block, hidden, rows_ref, *refs):
    gate_refs, up_refs = refs[:count], refs[count : 2 * count]
    grads_ref, terms_ref = refs[2 * count :]
    gate_sum, up_sum = 0.0, 0.0
    for i in range(count):
        part = rows_ref[:, i * block : (i + 1) * block]
        gate_sum = gate_sum + jnp.dot(part, gate_refs[i][...], preferred_element_type=jnp.float32)
        up_sum = up_sum + jnp.dot(part, up_refs[i][...], preferred_element_type=jnp.float32)
    sigma = 1.0 / (1.0 + jnp.exp(-gate_sum))
    scaled = rows_ref[:, count * block :].astype(jnp.float32)
    grad_gate = (scaled * up_sum * sigma * (1.0 + gate_sum * (1.0 - sigma))).astype(jnp.bfloat16)
    grad_up = (scaled * gate_sum * sigma).astype(jnp.bfloat16)
    grads_ref[:, :hidden] = grad_gate
    grads_ref[:, hidden:] = grad_up
    contract_cols = (((1,), (1,)), ((), ()))
    for i in range(count):
        terms_ref[:, i * block : (i + 1) * block] = (
            lax.dot_general(
                grad_gate, gate_refs[i][...], contract_cols, preferred_element_type=jnp.float32
            )
            + lax.dot_general(
                grad_up, up_refs[i][...], contract_cols, preferred_element_type=jnp.float32
            )
        ).astype(jnp.bfloat16)


def expert_rows(rows, gate_blocks, up_blocks):
    count = len(gate_blocks)
    block, hidden = gate_blocks[0].shape
    depth = rows.shape[0]
    in_vmem = pl.BlockSpec(memory_space=pltpu.VMEM)
    return pl.pallas_call(
        functools.partial(expert_kernel, count, block, hidden),
        out_shape=(
            jax.ShapeDtypeStruct((depth, 2 * hidden), jnp.bfloat16),
            jax.ShapeDtypeStruct((depth, count * block), jnp.bfloat16),
        ),
        in_specs=[in_vmem] * (1 + 2 * count),
        out_specs=(in_vmem, in_vmem),
        compiler_params=pltpu.CompilerParams(vmem_limit_bytes=32 << 20),
        cost_estimate=pl.CostEstimate(
            flops=8 * depth * hidden * count * block,
            bytes_accessed=4 * hidden * count * block + 4 * depth * (count * block + hidden),
            transcendentals=depth * hidden,
        ),
    )(rows, *gate_blocks, *up_blocks)


PLANE = 8


def exchange_kernel(
    total, send_ref, recv_ref, relay_ref, self_sem, send_sem, recv_sem, out_sem, in_sem, pass_sem
):
    me = lax.axis_index("expert")
    planes, half = total // PLANE, PLANE // 2
    plane, seat = me // PLANE, me % PLANE

    def device(step, place):
        return ((plane + step + planes) % planes) * PLANE + place

    def send(target):
        pltpu.make_async_remote_copy(
            src_ref=send_ref.at[target],
            dst_ref=recv_ref.at[me],
            send_sem=send_sem,
            recv_sem=recv_sem,
            device_id={"expert": target},
            device_id_type=pl.DeviceIdType.MESH,
        ).start()

    barrier = pltpu.get_barrier_semaphore()

    def greet(step, carry):
        pl.semaphore_signal(
            barrier,
            inc=1,
            device_id={"expert": (me + step) % total},
            device_id_type=pl.DeviceIdType.MESH,
        )
        return carry

    lax.fori_loop(1, total, greet, 0)
    pl.semaphore_wait(barrier, total - 1)

    relay = pltpu.make_async_remote_copy(
        src_ref=send_ref.at[pl.ds(device(planes // 2, half), half)],
        dst_ref=relay_ref,
        send_sem=out_sem,
        recv_sem=in_sem,
        device_id={"expert": device(-(planes // 4), seat)},
        device_id_type=pl.DeviceIdType.MESH,
    )
    relay.start()
    for place in range(half):
        send(device(planes // 2, place))
    own = pltpu.make_async_copy(send_ref.at[me], recv_ref.at[me], self_sem)
    own.start()

    def both_ways(item, carry):
        step = planes // 2 - 1 - item // PLANE
        place = (seat + item) % PLANE
        send(device(step, place))
        send(device(-step, place))
        return carry

    def same_plane(step, carry):
        send(device(0, (seat + step) % PLANE))
        return carry

    pairs = (planes // 2 - 1) * PLANE
    lax.fori_loop(0, pairs // 2, both_ways, 0)
    relay.wait_recv()
    source = device(planes // 4, seat)
    for place in range(half):
        pltpu.make_async_remote_copy(
            src_ref=relay_ref.at[place],
            dst_ref=recv_ref.at[source],
            send_sem=pass_sem,
            recv_sem=recv_sem,
            device_id={"expert": device(-(planes // 4), half + place)},
            device_id_type=pl.DeviceIdType.MESH,
        ).start()
    lax.fori_loop(pairs // 2, pairs, both_ways, 0)
    lax.fori_loop(1, PLANE, same_plane, 0)

    own.wait()
    relay.wait_send()
    pltpu.make_async_copy(relay_ref, relay_ref, pass_sem).wait()
    sent = send_ref.at[pl.ds(0, total - 1 - half)]
    pltpu.make_async_copy(sent, sent, send_sem).wait()
    landed = recv_ref.at[pl.ds(0, total - 1)]
    pltpu.make_async_copy(landed, landed, recv_sem).wait()


def exchange(pieces):
    total = pieces.shape[0]
    in_place = pl.BlockSpec(memory_space=pl.ANY)
    return pl.pallas_call(
        functools.partial(exchange_kernel, total),
        out_shape=jax.ShapeDtypeStruct(pieces.shape, pieces.dtype),
        in_specs=[in_place],
        out_specs=in_place,
        scratch_shapes=[pltpu.VMEM((PLANE // 2, *pieces.shape[1:]), pieces.dtype)]
        + [pltpu.SemaphoreType.DMA] * 6,
        compiler_params=pltpu.CompilerParams(
            collective_id=0, has_side_effects=True, vmem_limit_bytes=4 << 20
        ),
    )(pieces)


def per_device(tokens, hidden_grad, gate_prob, slot_choice, replica_plan, weights):
    expert_count = lax.axis_size("expert")
    group_count = lax.axis_size("dp")
    me = lax.axis_index("dp")
    token_count, pick_count = slot_choice.shape
    row_count = token_count * pick_count
    capacity = max(2, 2 * row_count // expert_count)
    depth_rows = expert_count * capacity
    model_width = tokens.shape[1]
    hidden_width = hidden_grad.shape[2]
    expert_total = weights.shape[0]
    shard_rows = weights.shape[2]
    block_rows = shard_rows * expert_count
    routed_width = model_width + hidden_width

    slots = jnp.arange(expert_count, dtype=jnp.int32)
    chooser = one_hot(replica_plan[:, None] == jnp.arange(expert_total, dtype=jnp.int32)[None, :])
    send_weights = jnp.einsum(
        "se,ekdf->skdf", chooser, weights, preferred_element_type=jnp.float32
    ).astype(jnp.bfloat16)
    own = lax.all_to_all(send_weights, "expert", split_axis=0, concat_axis=0, tiled=True)
    own_gate = own[:, 0].reshape(block_rows, hidden_width)
    own_up = own[:, 1].reshape(block_rows, hidden_width)
    left_gate = shift(own_gate, 1)
    right_up = shift(own_up, -1)
    left_up = shift(own_up, 1)
    right_gate = shift(own_gate, -1)
    far_gate = shift(left_gate, 1)
    far_up = shift(right_up, -1)
    gate_blocks = [own_gate, right_gate, far_gate, left_gate]
    up_blocks = [own_up, right_up, far_up, left_up]

    flat_slot = slot_choice.reshape(row_count)
    slot_member = (flat_slot[:, None] == slots[None, :]).astype(jnp.int32)
    ranking = jnp.sum((jnp.cumsum(slot_member, axis=0) - 1) * slot_member, axis=1)
    position = flat_slot * capacity + ranking
    scatter_table = one_hot(jnp.arange(depth_rows, dtype=jnp.int32)[:, None] == position[None, :])
    token_rows = jnp.repeat(rotate_columns(tokens, me, block_rows), pick_count, axis=0)
    cotangent = (gate_prob[:, :, None] * hidden_grad.astype(jnp.float32)).astype(jnp.bfloat16)
    cotangent = cotangent.reshape(row_count, hidden_width)
    routed = jnp.concatenate([token_rows, cotangent], axis=1)
    send_rows = jnp.dot(scatter_table, routed, preferred_element_type=jnp.float32).astype(
        jnp.bfloat16
    )
    send_rows, _ = lax.optimization_barrier(
        (send_rows.reshape(expert_count, capacity, routed_width), own)
    )
    rows = lax.all_to_all(
        send_rows, "expert", split_axis=0, concat_axis=0, tiled=True
    ).reshape(depth_rows, routed_width)

    grads, row_terms = expert_rows(rows, gate_blocks, up_blocks)
    back_rows = lax.all_to_all(
        row_terms.reshape(expert_count, capacity, model_width),
        "expert",
        split_axis=0,
        concat_axis=0,
        tiled=True,
    ).reshape(depth_rows, model_width)

    blocks = [rows[:, i * block_rows : (i + 1) * block_rows] for i in range(group_count)]
    columns = [blocks[0], shift(blocks[3], -1), shift(blocks[2], 2), shift(blocks[1], 1)]
    grads_left = shift(grads, 1)
    grads_right = shift(grads, -1)
    middle = depth_rows // 2
    grads_far = [shift(grads_left[:middle], 1), shift(grads_right[middle:], -1)]
    contract_rows = (((0,), (0,)), ((), ()))
    own_columns, right_columns, far_columns, left_columns = columns
    summed = jnp.float32(0.0)
    for column, grad in (
        (own_columns, grads),
        (left_columns, grads_left),
        (right_columns, grads_right),
        (far_columns[:middle], grads_far[0]),
        (far_columns[middle:], grads_far[1]),
    ):
        summed = lax.optimization_barrier(summed) + lax.dot_general(
            column, grad, contract_rows, preferred_element_type=jnp.float32
        )
    summed = summed.astype(jnp.bfloat16)
    pieces = summed.reshape(expert_count, shard_rows, 2, hidden_width).transpose(0, 2, 1, 3)
    gathered = exchange(pieces)
    membership = one_hot(
        jnp.arange(expert_total, dtype=jnp.int32)[:, None] == replica_plan[None, :]
    )
    expert_grad = jnp.einsum(
        "es,skdf->ekdf", membership, gathered, preferred_element_type=jnp.float32
    )
    expert_grad = (expert_grad / group_count).astype(jnp.bfloat16)

    token_grads = lax.dot_general(
        scatter_table, back_rows, contract_rows, preferred_element_type=jnp.float32
    )
    input_grad = jnp.sum(token_grads.reshape(token_count, pick_count, model_width), axis=1).astype(
        jnp.bfloat16
    )
    input_grad = rotate_columns(input_grad, (group_count - me) % group_count, block_rows)
    return (input_grad, expert_grad)


def solution(mesh):
    placed = (
        P(("dp", "expert"), None),
        P(("dp", "expert"), None, None),
        P(("dp", "expert"), None),
        P(("dp", "expert"), None),
        P(),
        P(None, None, ("dp", "expert"), None),
    )
    return jax.shard_map(
        per_device,
        mesh=mesh,
        in_specs=placed,
        out_specs=(P(("dp", "expert"), None), P(None, None, ("dp", "expert"), None)),
        check_vma=False,
    )
```

```python
import functools

import jax
import jax.numpy as jnp
from jax import lax
from jax.experimental import pallas as pl
from jax.experimental.pallas import tpu as pltpu
from jax.sharding import PartitionSpec as P


def shift(values, distance):
    size = lax.axis_size("dp")
    return lax.ppermute(values, "dp", [(i, (i + distance) % size) for i in range(size)])


def rotate_columns(values, start_block, block):
    doubled = jnp.concatenate([values, values], axis=1)
    return lax.dynamic_slice_in_dim(doubled, start_block * block, values.shape[1], axis=1)


def one_hot(condition):
    return condition.astype(jnp.bfloat16)


def expert_kernel(count, block, hidden, rows_ref, *refs):
    gate_refs, up_refs = refs[:count], refs[count : 2 * count]
    grads_ref, terms_ref = refs[2 * count :]
    gate_sum, up_sum = 0.0, 0.0
    for i in range(count):
        part = rows_ref[:, i * block : (i + 1) * block]
        gate_sum = gate_sum + jnp.dot(part, gate_refs[i][...], preferred_element_type=jnp.float32)
        up_sum = up_sum + jnp.dot(part, up_refs[i][...], preferred_element_type=jnp.float32)
    sigma = 1.0 / (1.0 + jnp.exp(-gate_sum))
    scaled = rows_ref[:, count * block :].astype(jnp.float32)
    grad_gate = (scaled * up_sum * sigma * (1.0 + gate_sum * (1.0 - sigma))).astype(jnp.bfloat16)
    grad_up = (scaled * gate_sum * sigma).astype(jnp.bfloat16)
    grads_ref[:, :hidden] = grad_gate
    grads_ref[:, hidden:] = grad_up
    contract_cols = (((1,), (1,)), ((), ()))
    for i in range(count):
        terms_ref[:, i * block : (i + 1) * block] = (
            lax.dot_general(
                grad_gate, gate_refs[i][...], contract_cols, preferred_element_type=jnp.float32
            )
            + lax.dot_general(
                grad_up, up_refs[i][...], contract_cols, preferred_element_type=jnp.float32
            )
        ).astype(jnp.bfloat16)


def expert_rows(rows, gate_blocks, up_blocks):
    count = len(gate_blocks)
    block, hidden = gate_blocks[0].shape
    depth = rows.shape[0]
    in_vmem = pl.BlockSpec(memory_space=pltpu.VMEM)
    return pl.pallas_call(
        functools.partial(expert_kernel, count, block, hidden),
        out_shape=(
            jax.ShapeDtypeStruct((depth, 2 * hidden), jnp.bfloat16),
            jax.ShapeDtypeStruct((depth, count * block), jnp.bfloat16),
        ),
        in_specs=[in_vmem] * (1 + 2 * count),
        out_specs=(in_vmem, in_vmem),
        compiler_params=pltpu.CompilerParams(vmem_limit_bytes=32 << 20),
        cost_estimate=pl.CostEstimate(
            flops=8 * depth * hidden * count * block,
            bytes_accessed=4 * hidden * count * block + 4 * depth * (count * block + hidden),
            transcendentals=depth * hidden,
        ),
    )(rows, *gate_blocks, *up_blocks)


PLANE = 8


def exchange_kernel(
    total, send_ref, recv_ref, relay_ref, self_sem, send_sem, recv_sem, out_sem, in_sem, pass_sem
):
    me = lax.axis_index("expert")
    planes, half = total // PLANE, PLANE // 2
    plane, seat = me // PLANE, me % PLANE

    def device(step, place):
        return ((plane + step + planes) % planes) * PLANE + place

    def send(target):
        pltpu.make_async_remote_copy(
            src_ref=send_ref.at[target],
            dst_ref=recv_ref.at[me],
            send_sem=send_sem,
            recv_sem=recv_sem,
            device_id={"expert": target},
            device_id_type=pl.DeviceIdType.MESH,
        ).start()

    barrier = pltpu.get_barrier_semaphore()

    def greet(step, carry):
        pl.semaphore_signal(
            barrier,
            inc=1,
            device_id={"expert": (me + step) % total},
            device_id_type=pl.DeviceIdType.MESH,
        )
        return carry

    lax.fori_loop(1, total, greet, 0)
    pl.semaphore_wait(barrier, total - 1)

    relay = pltpu.make_async_remote_copy(
        src_ref=send_ref.at[pl.ds(device(planes // 2, half), half)],
        dst_ref=relay_ref,
        send_sem=out_sem,
        recv_sem=in_sem,
        device_id={"expert": device(-(planes // 4), seat)},
        device_id_type=pl.DeviceIdType.MESH,
    )
    relay.start()
    for place in range(half):
        send(device(planes // 2, place))
    own = pltpu.make_async_copy(send_ref.at[me], recv_ref.at[me], self_sem)
    own.start()

    def both_ways(item, carry):
        step = planes // 2 - 1 - item // PLANE
        place = (seat + item) % PLANE
        send(device(step, place))
        send(device(-step, place))
        return carry

    def same_plane(step, carry):
        send(device(0, (seat + step) % PLANE))
        return carry

    pairs = (planes // 2 - 1) * PLANE
    lax.fori_loop(0, pairs // 4, both_ways, 0)
    relay.wait_recv()
    source = device(planes // 4, seat)
    for place in range(half):
        pltpu.make_async_remote_copy(
            src_ref=relay_ref.at[place],
            dst_ref=recv_ref.at[source],
            send_sem=pass_sem,
            recv_sem=recv_sem,
            device_id={"expert": device(-(planes // 4), half + place)},
            device_id_type=pl.DeviceIdType.MESH,
        ).start()
    lax.fori_loop(pairs // 4, pairs, both_ways, 0)
    lax.fori_loop(1, PLANE, same_plane, 0)

    own.wait()
    relay.wait_send()
    pltpu.make_async_copy(relay_ref, relay_ref, pass_sem).wait()
    sent = send_ref.at[pl.ds(0, total - 1 - half)]
    pltpu.make_async_copy(sent, sent, send_sem).wait()
    landed = recv_ref.at[pl.ds(0, total - 1)]
    pltpu.make_async_copy(landed, landed, recv_sem).wait()


def exchange(pieces):
    total = pieces.shape[0]
    in_place = pl.BlockSpec(memory_space=pl.ANY)
    return pl.pallas_call(
        functools.partial(exchange_kernel, total),
        out_shape=jax.ShapeDtypeStruct(pieces.shape, pieces.dtype),
        in_specs=[in_place],
        out_specs=in_place,
        scratch_shapes=[pltpu.VMEM((PLANE // 2, *pieces.shape[1:]), pieces.dtype)]
        + [pltpu.SemaphoreType.DMA] * 6,
        compiler_params=pltpu.CompilerParams(
            collective_id=0, has_side_effects=True, vmem_limit_bytes=4 << 20
        ),
    )(pieces)


def per_device(tokens, hidden_grad, gate_prob, slot_choice, replica_plan, weights):
    expert_count = lax.axis_size("expert")
    group_count = lax.axis_size("dp")
    me = lax.axis_index("dp")
    token_count, pick_count = slot_choice.shape
    row_count = token_count * pick_count
    capacity = max(2, 2 * row_count // expert_count)
    depth_rows = expert_count * capacity
    model_width = tokens.shape[1]
    hidden_width = hidden_grad.shape[2]
    expert_total = weights.shape[0]
    shard_rows = weights.shape[2]
    block_rows = shard_rows * expert_count
    routed_width = model_width + hidden_width

    slots = jnp.arange(expert_count, dtype=jnp.int32)
    chooser = one_hot(replica_plan[:, None] == jnp.arange(expert_total, dtype=jnp.int32)[None, :])
    send_weights = jnp.einsum(
        "se,ekdf->skdf", chooser, weights, preferred_element_type=jnp.float32
    ).astype(jnp.bfloat16)
    own = lax.all_to_all(send_weights, "expert", split_axis=0, concat_axis=0, tiled=True)
    own_gate = own[:, 0].reshape(block_rows, hidden_width)
    own_up = own[:, 1].reshape(block_rows, hidden_width)
    left_gate = shift(own_gate, 1)
    right_up = shift(own_up, -1)
    left_up = shift(own_up, 1)
    right_gate = shift(own_gate, -1)
    far_gate = shift(left_gate, 1)
    far_up = shift(right_up, -1)
    gate_blocks = [own_gate, right_gate, far_gate, left_gate]
    up_blocks = [own_up, right_up, far_up, left_up]

    flat_slot = slot_choice.reshape(row_count)
    slot_member = (flat_slot[:, None] == slots[None, :]).astype(jnp.int32)
    ranking = jnp.sum((jnp.cumsum(slot_member, axis=0) - 1) * slot_member, axis=1)
    position = flat_slot * capacity + ranking
    scatter_table = one_hot(jnp.arange(depth_rows, dtype=jnp.int32)[:, None] == position[None, :])
    token_rows = jnp.repeat(rotate_columns(tokens, me, block_rows), pick_count, axis=0)
    cotangent = (gate_prob[:, :, None] * hidden_grad.astype(jnp.float32)).astype(jnp.bfloat16)
    cotangent = cotangent.reshape(row_count, hidden_width)
    routed = jnp.concatenate([token_rows, cotangent], axis=1)
    send_rows = jnp.dot(scatter_table, routed, preferred_element_type=jnp.float32).astype(
        jnp.bfloat16
    )
    send_rows, _ = lax.optimization_barrier(
        (send_rows.reshape(expert_count, capacity, routed_width), own)
    )
    rows = lax.all_to_all(
        send_rows, "expert", split_axis=0, concat_axis=0, tiled=True
    ).reshape(depth_rows, routed_width)

    grads, row_terms = expert_rows(rows, gate_blocks, up_blocks)
    back_rows = lax.all_to_all(
        row_terms.reshape(expert_count, capacity, model_width),
        "expert",
        split_axis=0,
        concat_axis=0,
        tiled=True,
    ).reshape(depth_rows, model_width)

    blocks = [rows[:, i * block_rows : (i + 1) * block_rows] for i in range(group_count)]
    columns = [blocks[0], shift(blocks[3], -1), shift(blocks[2], 2), shift(blocks[1], 1)]
    grads_left = shift(grads, 1)
    grads_right = shift(grads, -1)
    middle = depth_rows // 2
    grads_far = [shift(grads_left[:middle], 1), shift(grads_right[middle:], -1)]
    contract_rows = (((0,), (0,)), ((), ()))
    own_columns, right_columns, far_columns, left_columns = columns
    summed = jnp.float32(0.0)
    for column, grad in (
        (own_columns, grads),
        (left_columns, grads_left),
        (right_columns, grads_right),
        (far_columns[:middle], grads_far[0]),
        (far_columns[middle:], grads_far[1]),
    ):
        summed = lax.optimization_barrier(summed) + lax.dot_general(
            column, grad, contract_rows, preferred_element_type=jnp.float32
        )
    summed = summed.astype(jnp.bfloat16)
    pieces = summed.reshape(expert_count, shard_rows, 2, hidden_width).transpose(0, 2, 1, 3)
    gathered = exchange(pieces)
    membership = one_hot(
        jnp.arange(expert_total, dtype=jnp.int32)[:, None] == replica_plan[None, :]
    )
    expert_grad = jnp.einsum(
        "es,skdf->ekdf", membership, gathered, preferred_element_type=jnp.float32
    )
    expert_grad = (expert_grad / group_count).astype(jnp.bfloat16)

    token_grads = lax.dot_general(
        scatter_table, back_rows, contract_rows, preferred_element_type=jnp.float32
    )
    input_grad = jnp.sum(token_grads.reshape(token_count, pick_count, model_width), axis=1).astype(
        jnp.bfloat16
    )
    input_grad = rotate_columns(input_grad, (group_count - me) % group_count, block_rows)
    return (input_grad, expert_grad)


def solution(mesh):
    placed = (
        P(("dp", "expert"), None),
        P(("dp", "expert"), None, None),
        P(("dp", "expert"), None),
        P(("dp", "expert"), None),
        P(),
        P(None, None, ("dp", "expert"), None),
    )
    return jax.shard_map(
        per_device,
        mesh=mesh,
        in_specs=placed,
        out_specs=(P(("dp", "expert"), None), P(None, None, ("dp", "expert"), None)),
        check_vma=False,
    )
```
